32 devices in a mesh: row: 8 (over z, y), col: 4 (over x, core).
Axes of the slice: x: 2, y: 2, z: 4, core: 2. Of those that a mesh axis runs over, the one named last changes fastest.
Arguments:
- dens_alpha: bfloat16 [2048, 2048], P('row', 'col'), may hold values from -6 to 6
- dens_beta: bfloat16 [2048, 2048], P('row', 'col'), may hold values from -6 to 6
- integrals: bfloat16 [512, 256, 256], P(('row', 'col')), may hold values from -0.375 to 0.375
- tile_quartet: int32 [512, 4], P(('row', 'col')), may hold values from 0 to 127, as said below
- tile_count: int32 [32], P(('row', 'col')), may hold values from 2 to 16, as said below
Outputs:
- fock_alpha: float32 [2048, 2048], P('row', 'col')
- fock_beta: float32 [2048, 2048], P('row', 'col')
The draws below stay inside these ranges and needn't reach their ends.
Inputs may be any that keep to these rules, and one draw needn't show every extreme that they name: `tile_quartet`: slots d * 16 to d * 16 + 15 belong to device d = i * 4 + j (i its row index, j its col index). Each row holds block indices P, Q, R, S of 16 functions; Q lies in i * 16 up to but excluding (i + 1) * 16, and R in j * 32 up to but excluding (j + 1) * 32; S may be any block. Among the 16 slots of one device, exactly 2 have P in each range k * 16 up to but excluding (k + 1) * 16, and so exactly 4 in each range of width 2048 // 64; their order within the device is arbitrary. `tile_count`: the live slots of a device are its first ones; some device has all 16 live.
All inputs are finite; a program needn't handle non-finite values.
Results may differ from the reference program's by a relative error of at most 0.0026.
Values may be sent and summed in bfloat16 or wider, within the bound.
No kernel may reach another device: no remote copies, remote signals or barrier semaphores. Data moves between devices by JAX's collectives and lax.ppermute only.
A program may use at most 128 MiB of HBM per device.

```python
import jax
import jax.numpy as jnp
from jax import lax

NBASIS = 2048
SHELL = 16
SLOTS = 16
TILES = 512
N_ROW = 8
N_COL = 4


def draw_tile_count(key, part):
    device_total = N_ROW * N_COL
    key_div, key_full = jax.random.split(jax.random.fold_in(key, 11))
    divisor = jax.random.randint(key_div, (device_total,), 1, 9)
    counts = SLOTS // divisor
    full_device = jax.random.randint(key_full, (), 0, device_total)
    return jnp.where(jnp.arange(device_total) == full_device, SLOTS, counts).astype(jnp.int32)


def draw_tile_quartet(key, part):
    keys = jax.random.split(jax.random.fold_in(key, 23), 7)
    device_total = N_ROW * N_COL
    total = device_total * SLOTS
    device = jnp.arange(total, dtype=jnp.int32) // SLOTS
    row_blocks = NBASIS // (N_ROW * SHELL)
    col_blocks = NBASIS // (N_COL * SHELL)
    all_blocks = NBASIS // SHELL
    ratio = N_ROW // N_COL
    base = jnp.broadcast_to(jnp.arange(SLOTS, dtype=jnp.int32)[None, :], (device_total, SLOTS))
    shuffled = jax.random.permutation(keys[4], base, axis=1, independent=True).reshape(total)
    offset_col = jax.random.randint(keys[5], (device_total,), 0, N_COL)[device]
    offset_sub = jax.random.randint(keys[6], (device_total,), 0, ratio)[device]
    dest_col = (shuffled + offset_col) % N_COL
    dest_sub = (shuffled // N_COL + offset_sub) % ratio
    dest_row = dest_col * ratio + dest_sub
    index_p = dest_row * row_blocks + jax.random.randint(keys[0], (total,), 0, row_blocks)
    index_q = device // N_COL * row_blocks + jax.random.randint(keys[1], (total,), 0, row_blocks)
    index_r = device % N_COL * col_blocks + jax.random.randint(keys[2], (total,), 0, col_blocks)
    index_s = jax.random.randint(keys[3], (total,), 0, all_blocks)
    return jnp.stack([index_p, index_q, index_r, index_s], 1).astype(jnp.int32)


def shard_levels(key, shape, shards, low, high):
    level = 1.0
    for position, parts in shards:
        steps = jax.random.uniform(jax.random.fold_in(jax.random.fold_in(key, 6), position), (parts,), jnp.float32, low / len(shards), high / len(shards))
        level = level * jnp.repeat(jnp.exp(steps), shape[position] // parts).reshape((-1,) + (1,) * (len(shape) - 1 - position))
    return level


def centred(own_key, shape, scale, most, shards=(), held_as=jnp.bfloat16):
    gain = shard_levels(own_key, shape, shards, -0.22, 0.18) if shards else 1.0
    entries = jax.random.normal(own_key, shape, jnp.float32) * scale * gain
    return jnp.minimum(jnp.maximum(entries, -most), most).astype(held_as)


def setup_inputs(seed: int = 0) -> dict:
    key_list = jax.random.split(jax.random.key(seed), 6)
    return {
        "dens_alpha": centred(key_list[0], (NBASIS, NBASIS), 1.0, 6.0, ((0, 8), (1, 4))),
        "dens_beta": centred(key_list[1], (NBASIS, NBASIS), 1.0, 6.0, ((0, 8), (1, 4))),
        "integrals": centred(key_list[2], (TILES, SHELL * SHELL, SHELL * SHELL), (SHELL * SHELL) ** -0.5, 0.375, ((0, 32),)),
        "tile_quartet": draw_tile_quartet(jax.random.fold_in(key_list[5], 71), 0),
        "tile_count": draw_tile_count(jax.random.fold_in(key_list[5], 71), 0),
    }


def reference(dens_alpha, dens_beta, integrals, tile_quartet, tile_count):
    block_count = NBASIS // SHELL
    summed = (dens_alpha.astype(jnp.float32) + dens_beta.astype(jnp.float32)).astype(jnp.bfloat16)
    summed_view = summed.reshape(block_count, SHELL, block_count, SHELL)
    alpha_view = dens_alpha.reshape(block_count, SHELL, block_count, SHELL)
    beta_view = dens_beta.reshape(block_count, SHELL, block_count, SHELL)
    offsets = jnp.arange(SHELL, dtype=jnp.int32)

    def visit(totals, device):
        coulomb, exch_alpha, exch_beta = totals
        first_slot = (device * SLOTS).astype(jnp.int32)
        tile_data = lax.dynamic_slice_in_dim(integrals, first_slot, SLOTS, 0).astype(jnp.float32)
        tile_data = tile_data.reshape(SLOTS, SHELL, SHELL, SHELL, SHELL)
        quartets = lax.dynamic_slice_in_dim(tile_quartet, first_slot, SLOTS, 0)
        index_p = quartets[:, 0]
        index_q = quartets[:, 1]
        index_r = quartets[:, 2]
        index_s = quartets[:, 3]
        live_mask = (jnp.arange(SLOTS, dtype=jnp.int32) < tile_count[device]).astype(jnp.float32)[:, None, None]
        coul_dens = summed_view[index_s, :, index_r, :].astype(jnp.float32)
        alpha_dens = alpha_view[index_q, :, index_s, :].astype(jnp.float32)
        beta_dens = beta_view[index_q, :, index_s, :].astype(jnp.float32)
        coul_part = jnp.einsum('tpqrs,tsr->tqp', tile_data, coul_dens) * live_mask
        alpha_part = jnp.einsum('tpqrs,tqs->tpr', tile_data, alpha_dens) * live_mask
        beta_part = jnp.einsum('tpqrs,tqs->tpr', tile_data, beta_dens) * live_mask
        rows_q = index_q[:, None, None] * SHELL + offsets[None, :, None]
        cols_p = index_p[:, None, None] * SHELL + offsets[None, None, :]
        coulomb = coulomb.at[rows_q, cols_p].add(coul_part)
        rows_p = index_p[:, None, None] * SHELL + offsets[None, :, None]
        cols_r = index_r[:, None, None] * SHELL + offsets[None, None, :]
        exch_alpha = exch_alpha.at[rows_p, cols_r].add(alpha_part)
        exch_beta = exch_beta.at[rows_p, cols_r].add(beta_part)
        return (coulomb, exch_alpha, exch_beta), None

    empty_fock = jnp.zeros((NBASIS, NBASIS), jnp.float32)
    devices = jnp.arange(N_ROW * N_COL, dtype=jnp.int32)
    (coulomb, exch_alpha, exch_beta), unused = lax.scan(visit, (empty_fock, empty_fock, empty_fock), devices)
    return coulomb - exch_alpha, coulomb - exch_beta
```

```python
import jax
import jax.numpy as jnp
from jax import lax
from jax.experimental import pallas as pl
from jax.experimental.pallas import tpu as pltpu
from jax.sharding import PartitionSpec as P

SHELL = 16
LANES = 128
PER = LANES // SHELL
UNROLL = 4
F32 = jnp.float32
BF16 = jnp.bfloat16
I32 = jnp.int32


def iota(shape, axis):
    return lax.broadcasted_iota(I32, shape, axis)


def turn(x, dest, origin):
    return pltpu.roll(x, jnp.asarray(((dest - origin) * SHELL) & (LANES - 1), I32), 1)


def rows_at(block):
    return pl.ds(pl.multiple_of(block * SHELL, SHELL), SHELL)


def lanes_at(block):
    return pl.ds(pl.multiple_of((block // PER) * LANES, LANES), LANES)


def call(body, **kw):
    return pl.pallas_call(
        body, compiler_params=pltpu.CompilerParams(vmem_limit_bytes=32 * 2**20), **kw
    )


def smem():
    return pl.BlockSpec(memory_space=pltpu.SMEM)


def vmem():
    return pl.BlockSpec(memory_space=pltpu.VMEM)


def serve(dens_alpha, dens_beta, asked_row, asked_col, slots):
    rows_dev, cols_dev = dens_alpha.shape
    row_blocks, col_blocks = rows_dev // SHELL, cols_dev // SHELL
    n_row, n_col = asked_row.shape[0], len(asked_col)
    groups = slots // PER

    def body(*refs):
        a_ref, b_ref, ask_row = refs[:3]
        ask_col = refs[3 : 3 + n_col]
        out_row = refs[3 + n_col]
        out_col = refs[4 + n_col :]
        my_row, my_col = lax.axis_index("row"), lax.axis_index("col")
        place = iota((SHELL, LANES), 1) // SHELL

        def to_row(src, carry):
            for g in range(groups):
                acc = jnp.zeros((SHELL, LANES), F32)
                for k in range(PER):
                    t = g * PER + k
                    blk_r = ask_row[src, t * 4 + 2] - my_col * col_blocks
                    blk_s = ask_row[src, t * 4 + 3] - my_row * row_blocks
                    mine = jnp.logical_and(blk_s >= 0, blk_s < row_blocks)
                    at = (rows_at(jnp.where(mine, blk_s, 0)), lanes_at(blk_r))
                    both = (a_ref[at].astype(F32) + b_ref[at].astype(F32)).astype(BF16)
                    moved = turn(both.astype(F32), k, blk_r & (PER - 1))
                    acc = jnp.where(place == jnp.where(mine, k, -1), moved, acc)
                out_row[src, g * SHELL : (g + 1) * SHELL, :] = acc.astype(BF16)
            return carry

        lax.fori_loop(0, n_row, to_row, 0)
        for m in range(n_col):

            def to_col(g, carry, m=m):
                acc_a = jnp.zeros((SHELL, LANES), F32)
                acc_b = jnp.zeros((SHELL, LANES), F32)
                for k in range(PER):
                    t = g * PER + k
                    blk_q = ask_col[m][0, t * 4 + 1] - my_row * row_blocks
                    blk_s = ask_col[m][0, t * 4 + 3] - my_col * col_blocks
                    mine = jnp.logical_and(blk_s >= 0, blk_s < col_blocks)
                    blk_s = jnp.where(mine, blk_s, 0)
                    at = (rows_at(blk_q), lanes_at(blk_s))
                    keep = place == jnp.where(mine, k, -1)
                    off = blk_s & (PER - 1)
                    acc_a = jnp.where(keep, turn(a_ref[at].astype(F32), k, off), acc_a)
                    acc_b = jnp.where(keep, turn(b_ref[at].astype(F32), k, off), acc_b)
                out_col[m][rows_at(g), :] = acc_a.astype(BF16)
                out_col[m][rows_at(groups + g), :] = acc_b.astype(BF16)
                return carry

            lax.fori_loop(0, groups, to_col, 0)

    outs = call(
        body,
        in_specs=[vmem(), vmem()] + [smem()] * (1 + n_col),
        out_specs=[vmem()] * (1 + n_col),
        out_shape=[jax.ShapeDtypeStruct((n_row, groups * SHELL, LANES), BF16)]
        + [jax.ShapeDtypeStruct((2 * groups * SHELL, LANES), BF16)] * n_col,
        name="serve",
    )(dens_alpha, dens_beta, asked_row, *asked_col)
    return outs[0], outs[1:]


def two_pass(x, ones):
    high = x.astype(BF16)
    low = (x - high.astype(F32)).astype(BF16)
    return jnp.dot(high, ones, preferred_element_type=F32) + jnp.dot(
        low, ones, preferred_element_type=F32
    )


def contract(integrals, tile_count, own, got_row, got_col, row_blocks, col_blocks):
    slots, pair = integrals.shape[0], integrals.shape[1]
    n_row, n_col = got_row.shape[0], len(got_col)
    groups = slots // PER
    cap_row, cap_col = slots // n_row, slots // n_col
    rows_k = -(-cap_row * 2 // PER) * SHELL
    rows_j = -(-cap_col // PER) * SHELL

    def body(*refs):
        g_hbm, count_ref, own_ref, got_row_ref = refs[:4]
        got_col_ref = refs[4 : 4 + n_col]
        k_out = refs[4 + n_col]
        j_out = refs[5 + n_col : 5 + 2 * n_col]
        g_ref, sems, a_ref, v_ref, kp_ref, jp_ref, perm_ref, ranks = refs[5 + 2 * n_col :]
        count = jnp.minimum(count_ref[0], slots)
        steps = (count + UNROLL - 1) // UNROLL

        def copy(n):
            at = pl.ds(n * UNROLL, UNROLL)
            return pltpu.make_async_copy(g_hbm.at[at], g_ref.at[at], sems.at[n])

        def start(n, carry):
            copy(n).start()
            return carry

        lax.fori_loop(0, steps, start, 0)
        my_col = lax.axis_index("col")
        place = iota((SHELL, LANES), 1) // SHELL
        k_out[...] = jnp.zeros(k_out.shape, F32)
        for m in range(n_col):
            j_out[m][...] = jnp.zeros(j_out[m].shape, F32)
        for n in range(n_row + n_col):
            ranks[n] = 0
        summed = got_row_ref[0].astype(F32)
        for n in range(1, n_row):
            summed = summed + got_row_ref[n].astype(F32)
        spins = got_col_ref[0][...].astype(F32)
        for n in range(1, n_col):
            spins = spins + got_col_ref[n][...].astype(F32)
        summed16 = summed.astype(BF16)
        lane_row = iota((LANES, pair), 0)
        lane_col = iota((LANES, pair), 1)
        diag = (iota((SHELL, pair), 1) & (SHELL - 1)) == iota((SHELL, pair), 0)
        for k in range(PER):
            spread = (lane_row == k * SHELL + lane_col // SHELL).astype(F32).astype(BF16)
            wide = jnp.dot(summed16, spread, preferred_element_type=F32)
            for g in range(groups):
                t = g * PER + k
                piece = jnp.where(diag, wide[g * SHELL : (g + 1) * SHELL], 0.0)
                v_ref[t : t + 1, :] = jnp.sum(piece, axis=0, keepdims=True)
                for x in range(2):
                    first = (x * groups + g) * SHELL
                    y = jnp.where(place == k, spins[first : first + SHELL], 0.0)
                    for step in (64, 32, 16):
                        y = y + pltpu.roll(y, step, 1)
                    a_ref[x, t] = y
        big_row = iota((pair, pair), 0)
        big_col = iota((pair, pair), 1)
        swapped = (big_col & (SHELL - 1)) * SHELL + big_col // SHELL
        perm_ref[...] = (big_row == swapped).astype(F32).astype(BF16)

        def visit(n, carry):
            copy(n).wait()
            for u in range(UNROLL):
                t = n * UNROLL + u
                tile = g_ref[t]
                vec = jnp.broadcast_to(v_ref[pl.ds(t, 1), :], (SHELL, pair)).astype(BF16)
                row = lax.dot_general(
                    vec, tile, (((1,), (1,)), ((), ())), preferred_element_type=F32
                )
                jp_ref[rows_at(t), :] = jnp.where(diag, row, 0.0)
                by_q = jnp.dot(perm_ref[...], tile, preferred_element_type=F32)
                for x in range(2):
                    acc = [jnp.zeros((SHELL, LANES), F32) for _ in range(pair // LANES)]
                    for q in range(SHELL):
                        a_row = a_ref[x, t, q : q + 1, :]
                        for h in range(pair // LANES):
                            acc[h] = acc[h] + a_row * by_q[
                                q * SHELL : (q + 1) * SHELL, h * LANES : (h + 1) * LANES
                            ]
                    for h in range(pair // LANES):
                        kp_ref[rows_at(t * 2 + x), h * LANES : (h + 1) * LANES] = acc[h]
            return carry

        lax.fori_loop(0, steps, visit, 0)
        gather = (
            (iota((pair, LANES), 1) & (SHELL - 1)) == iota((pair, LANES), 0) // SHELL
        ).astype(F32).astype(BF16)

        def fold(n, carry):
            size = UNROLL * SHELL
            at_j = pl.ds(pl.multiple_of(n * size, size), size)
            at_k = pl.ds(pl.multiple_of(n * 2 * size, 2 * size), 2 * size)
            jj = two_pass(jp_ref[at_j, :], gather)
            kk = two_pass(kp_ref[at_k, :], gather)
            for u in range(UNROLL):
                t = n * UNROLL + u

                @pl.when(t < count)
                def _(u=u, t=t):
                    blk_p = own_ref[0, t * 4]
                    to = blk_p // row_blocks
                    rank = ranks[to]
                    ranks[to] = rank + 1
                    for x in range(2):
                        spot = rank * 2 + x
                        at = rows_at(spot // PER)
                        mine = kk[(u * 2 + x) * SHELL : (u * 2 + x + 1) * SHELL]
                        old = k_out[to, at, :]
                        k_out[to, at, :] = jnp.where(place == spot % PER, mine, old)
                    aim = blk_p // col_blocks
                    rank_c = ranks[n_row + aim]
                    ranks[n_row + aim] = rank_c + 1
                    way = lax.rem(aim - my_col + n_col, n_col)
                    at = rows_at(rank_c // PER)
                    mine = jj[u * SHELL : (u + 1) * SHELL]
                    for m in range(n_col):

                        @pl.when(way == m)
                        def _(m=m):
                            old = j_out[m][at, :]
                            j_out[m][at, :] = jnp.where(place == rank_c % PER, mine, old)

            return carry

        lax.fori_loop(0, steps, fold, 0)

    outs = call(
        body,
        in_specs=[pl.BlockSpec(memory_space=pl.ANY), smem(), smem()] + [vmem()] * (1 + n_col),
        out_specs=[vmem()] * (1 + n_col),
        out_shape=[jax.ShapeDtypeStruct((n_row, rows_k, LANES), F32)]
        + [jax.ShapeDtypeStruct((rows_j, LANES), F32)] * n_col,
        scratch_shapes=[
            pltpu.VMEM((slots, pair, pair), BF16),
            pltpu.SemaphoreType.DMA((slots // UNROLL,)),
            pltpu.VMEM((2, slots, SHELL, LANES), F32),
            pltpu.VMEM((slots, pair), F32),
            pltpu.VMEM((slots * 2 * SHELL, pair), F32),
            pltpu.VMEM((slots * SHELL, pair), F32),
            pltpu.VMEM((pair, pair), BF16),
            pltpu.SMEM((n_row + n_col,), I32),
        ],
        name="contract",
    )(integrals, tile_count, own, got_row, *got_col)
    return outs[0], outs[1:]


def assemble(k_got, j_got, asked_row, asked_col, slots, shape):
    row_blocks, col_blocks = shape[0] // SHELL, shape[1] // SHELL
    n_row, n_col = k_got.shape[0], len(j_got)

    def body(*refs):
        k_ref, ask_row = refs[:2]
        j_ref = refs[2 : 2 + n_col]
        ask_col = refs[2 + n_col : 2 + 2 * n_col]
        out_a, out_b = refs[2 + 2 * n_col :]
        my_row, my_col = lax.axis_index("row"), lax.axis_index("col")
        place = iota((SHELL, LANES), 1) // SHELL
        out_a[...] = jnp.zeros(shape, F32)
        out_b[...] = jnp.zeros(shape, F32)

        for m in range(n_col):

            def coulomb(t, rank, m=m):
                blk_p = ask_col[m][0, t * 4] - my_col * col_blocks
                blk_q = ask_col[m][0, t * 4 + 1] - my_row * row_blocks
                mine = jnp.logical_and(blk_p >= 0, blk_p < col_blocks)

                @pl.when(mine)
                def _():
                    off = blk_p & (PER - 1)
                    piece = turn(j_ref[m][rows_at(rank // PER), :], off, rank % PER)
                    piece = jnp.where(place == off, piece, 0.0)
                    at = (rows_at(blk_q), lanes_at(blk_p))
                    out_a[at] = out_a[at] + piece
                    out_b[at] = out_b[at] + piece

                return rank + mine.astype(I32)

            lax.fori_loop(0, slots, coulomb, jnp.int32(0), unroll=4)

        def source(src, carry):
            def exchange(t, rank):
                blk_p = ask_row[src, t * 4] - my_row * row_blocks
                blk_r = ask_row[src, t * 4 + 2] - my_col * col_blocks
                mine = jnp.logical_and(blk_p >= 0, blk_p < row_blocks)

                @pl.when(mine)
                def _():
                    off = blk_r & (PER - 1)
                    at = (rows_at(blk_p), lanes_at(blk_r))
                    for x, out in ((0, out_a), (1, out_b)):
                        spot = rank * 2 + x
                        piece = turn(k_ref[src, rows_at(spot // PER), :], off, spot % PER)
                        out[at] = out[at] - jnp.where(place == off, piece, 0.0)

                return rank + mine.astype(I32)

            lax.fori_loop(0, slots, exchange, jnp.int32(0), unroll=4)
            return carry

        lax.fori_loop(0, n_row, source, 0)

    return call(
        body,
        in_specs=[vmem(), smem()] + [vmem()] * n_col + [smem()] * n_col,
        out_specs=[vmem(), vmem()],
        out_shape=[jax.ShapeDtypeStruct(shape, F32)] * 2,
        name="assemble",
    )(k_got, asked_row, *j_got, *asked_col)


def shift(x, step, size):
    return lax.ppermute(x, "col", [(n, (n + step) % size) for n in range(size)])


def swap(x):
    return lax.all_to_all(x, "row", split_axis=0, concat_axis=0, tiled=True)


def local(dens_alpha, dens_beta, integrals, tile_quartet, tile_count):
    slots = integrals.shape[0]
    n_row, n_col = lax.axis_size("row"), lax.axis_size("col")
    row_blocks, col_blocks = dens_alpha.shape[0] // SHELL, dens_alpha.shape[1] // SHELL
    flat = tile_quartet.reshape(1, slots * 4)
    own = jnp.pad(flat, ((0, 0), (0, -(slots * 4) % LANES)))
    asked_col = [own] + [shift(own, m, n_col) for m in range(1, n_col)]
    asked_row = swap(jnp.broadcast_to(own, (n_row, own.shape[1])))
    to_row, to_col = serve(dens_alpha, dens_beta, asked_row, asked_col, slots)
    got_col = [to_col[0]] + [shift(to_col[m], -m, n_col) for m in range(1, n_col)]
    got_row = swap(to_row)
    k_send, j_send = contract(
        integrals, tile_count, own, got_row, got_col, row_blocks, col_blocks
    )
    j_got = [j_send[0]] + [shift(j_send[m], m, n_col) for m in range(1, n_col)]
    k_got = swap(k_send)
    out_a, out_b = assemble(k_got, j_got, asked_row, asked_col, slots, dens_alpha.shape)
    return (out_a, out_b)


def solution(mesh):
    in_specs = (
        P("row", "col"),
        P("row", "col"),
        P(("row", "col"), None, None),
        P(("row", "col"), None),
        P(("row", "col")),
    )
    out_specs = (P("row", "col"), P("row", "col"))
    return jax.shard_map(local, mesh=mesh, in_specs=in_specs, out_specs=out_specs, check_vma=False)
```

```python
import jax
import jax.numpy as jnp
from jax import lax
from jax.experimental import pallas as pl
from jax.experimental.pallas import tpu as pltpu
from jax.sharding import PartitionSpec as P


SHELL = 16
LANES = 128
PER = LANES // SHELL
UNROLL = 4
F32 = jnp.float32
BF16 = jnp.bfloat16
I32 = jnp.int32


def iota(shape, axis):
    return lax.broadcasted_iota(I32, shape, axis)


def turn(x, dest, origin):
    return pltpu.roll(x, jnp.asarray(((dest - origin) * SHELL) & (LANES - 1), I32), 1)


def rows_at(block):
    return pl.ds(pl.multiple_of(block * SHELL, SHELL), SHELL)


def lanes_at(block):
    return pl.ds(pl.multiple_of((block // PER) * LANES, LANES), LANES)


def call(body, **kw):
    return pl.pallas_call(
        body, compiler_params=pltpu.CompilerParams(vmem_limit_bytes=32 * 2**20), **kw
    )


def smem():
    return pl.BlockSpec(memory_space=pltpu.SMEM)


def vmem():
    return pl.BlockSpec(memory_space=pltpu.VMEM)


def serve(dens_alpha, dens_beta, asked_row, asked_col, slots):
    rows_dev, cols_dev = dens_alpha.shape
    row_blocks, col_blocks = rows_dev // SHELL, cols_dev // SHELL
    n_row, n_col = asked_row.shape[0], len(asked_col)
    groups = slots // PER

    def body(*refs):
        a_ref, b_ref, ask_row = refs[:3]
        ask_col = refs[3 : 3 + n_col]
        out_row = refs[3 + n_col]
        out_col = refs[4 + n_col :]
        my_row, my_col = lax.axis_index("row"), lax.axis_index("col")
        place = iota((SHELL, LANES), 1) // SHELL
        out_row[...] = jnp.zeros(out_row.shape, BF16)
        for m in range(n_col):
            out_col[m][...] = jnp.zeros(out_col[m].shape, BF16)

        def put(ref, at, keep, new):
            ref[at] = jnp.where(keep, new, ref[at].astype(F32)).astype(BF16)

        def to_row(src, carry):
            for t in range(slots):
                blk_s = ask_row[src, t * 4 + 3] - my_row * row_blocks

                @pl.when(jnp.logical_and(blk_s >= 0, blk_s < row_blocks))
                def _(t=t, blk_s=blk_s):
                    blk_r = ask_row[src, t * 4 + 2] - my_col * col_blocks
                    at = (rows_at(blk_s), lanes_at(blk_r))
                    both = (a_ref[at].astype(F32) + b_ref[at].astype(F32)).astype(BF16)
                    moved = turn(both.astype(F32), t % PER, blk_r & (PER - 1))
                    put(out_row, (src, rows_at(t // PER)), place == t % PER, moved)

            return carry

        lax.fori_loop(0, n_row, to_row, 0)
        for m in range(n_col):

            def to_col(g, carry, m=m):
                for k in range(PER):
                    t = g * PER + k
                    blk_s = ask_col[m][0, t * 4 + 3] - my_col * col_blocks

                    @pl.when(jnp.logical_and(blk_s >= 0, blk_s < col_blocks))
                    def _(t=t, k=k, blk_s=blk_s):
                        blk_q = ask_col[m][0, t * 4 + 1] - my_row * row_blocks
                        at = (rows_at(blk_q), lanes_at(blk_s))
                        off = blk_s & (PER - 1)
                        keep = place == k
                        moved_a = turn(a_ref[at].astype(F32), k, off)
                        moved_b = turn(b_ref[at].astype(F32), k, off)
                        put(out_col[m], (rows_at(g),), keep, moved_a)
                        put(out_col[m], (rows_at(groups + g),), keep, moved_b)

                return carry

            lax.fori_loop(0, groups, to_col, 0)

    outs = call(
        body,
        in_specs=[vmem(), vmem()] + [smem()] * (1 + n_col),
        out_specs=[vmem()] * (1 + n_col),
        out_shape=[jax.ShapeDtypeStruct((n_row, groups * SHELL, LANES), BF16)]
        + [jax.ShapeDtypeStruct((2 * groups * SHELL, LANES), BF16)] * n_col,
        name="serve",
    )(dens_alpha, dens_beta, asked_row, *asked_col)
    return outs[0], outs[1:]


def two_pass(x, ones):
    high = x.astype(BF16)
    low = (x - high.astype(F32)).astype(BF16)
    return jnp.dot(high, ones, preferred_element_type=F32) + jnp.dot(
        low, ones, preferred_element_type=F32
    )


def contract(integrals, tile_count, own, got_row, got_col, row_blocks, col_blocks):
    slots, pair = integrals.shape[0], integrals.shape[1]
    n_row, n_col = got_row.shape[0], len(got_col)
    groups = slots // PER
    cap_row, cap_col = slots // n_row, slots // n_col
    rows_k = -(-cap_row * 2 // PER) * SHELL
    rows_j = -(-cap_col // PER) * SHELL

    def body(*refs):
        g_ref, count_ref, own_ref, got_row_ref = refs[:4]
        got_col_ref = refs[4 : 4 + n_col]
        k_out = refs[4 + n_col]
        j_out = refs[5 + n_col : 5 + 2 * n_col]
        a_ref, v_ref, kp_ref, jp_ref, perm_ref, ranks = refs[5 + 2 * n_col :]
        count = jnp.minimum(count_ref[0], slots)
        steps = (count + UNROLL - 1) // UNROLL

        my_col = lax.axis_index("col")
        place = iota((SHELL, LANES), 1) // SHELL
        k_out[...] = jnp.zeros(k_out.shape, F32)
        for m in range(n_col):
            j_out[m][...] = jnp.zeros(j_out[m].shape, F32)
        for n in range(n_row + n_col):
            ranks[n] = 0
        summed = got_row_ref[0].astype(F32)
        for n in range(1, n_row):
            summed = summed + got_row_ref[n].astype(F32)
        spins = got_col_ref[0][...].astype(F32)
        for n in range(1, n_col):
            spins = spins + got_col_ref[n][...].astype(F32)
        summed16 = summed.astype(BF16)
        lane_row = iota((LANES, pair), 0)
        lane_col = iota((LANES, pair), 1)
        diag = (iota((SHELL, pair), 1) & (SHELL - 1)) == iota((SHELL, pair), 0)
        for k in range(PER):
            spread = (lane_row == k * SHELL + lane_col // SHELL).astype(F32).astype(BF16)
            wide = jnp.dot(summed16, spread, preferred_element_type=F32)
            for g in range(groups):
                t = g * PER + k
                piece = jnp.where(diag, wide[g * SHELL : (g + 1) * SHELL], 0.0)
                v_ref[t : t + 1, :] = jnp.sum(piece, axis=0, keepdims=True)
                for x in range(2):
                    first = (x * groups + g) * SHELL
                    y = jnp.where(place == k, spins[first : first + SHELL], 0.0)
                    for step in (64, 32, 16):
                        y = y + pltpu.roll(y, step, 1)
                    a_ref[x, t] = y
        big_row = iota((pair, pair), 0)
        big_col = iota((pair, pair), 1)
        swapped = (big_col & (SHELL - 1)) * SHELL + big_col // SHELL
        perm_ref[...] = (big_row == swapped).astype(F32).astype(BF16)

        def visit(n, carry):
            for u in range(UNROLL):
                t = n * UNROLL + u
                tile = g_ref[t]
                vec = jnp.broadcast_to(v_ref[pl.ds(t, 1), :], (SHELL, pair)).astype(BF16)
                row = lax.dot_general(
                    vec, tile, (((1,), (1,)), ((), ())), preferred_element_type=F32
                )
                jp_ref[rows_at(t), :] = jnp.where(diag, row, 0.0)
                by_q = jnp.dot(perm_ref[...], tile, preferred_element_type=F32)
                for x in range(2):
                    acc = [jnp.zeros((SHELL, LANES), F32) for _ in range(pair // LANES)]
                    for q in range(SHELL):
                        a_row = a_ref[x, t, q : q + 1, :]
                        for h in range(pair // LANES):
                            acc[h] = acc[h] + a_row * by_q[
                                q * SHELL : (q + 1) * SHELL, h * LANES : (h + 1) * LANES
                            ]
                    for h in range(pair // LANES):
                        kp_ref[rows_at(t * 2 + x), h * LANES : (h + 1) * LANES] = acc[h]
            return carry

        lax.fori_loop(0, steps, visit, 0)
        gather = (
            (iota((pair, LANES), 1) & (SHELL - 1)) == iota((pair, LANES), 0) // SHELL
        ).astype(F32).astype(BF16)

        def fold(n, carry):
            size = UNROLL * SHELL
            at_j = pl.ds(pl.multiple_of(n * size, size), size)
            at_k = pl.ds(pl.multiple_of(n * 2 * size, 2 * size), 2 * size)
            jj = two_pass(jp_ref[at_j, :], gather)
            kk = two_pass(kp_ref[at_k, :], gather)
            for u in range(UNROLL):
                t = n * UNROLL + u

                @pl.when(t < count)
                def _(u=u, t=t):
                    blk_p = own_ref[0, t * 4]
                    to = blk_p // row_blocks
                    rank = ranks[to]
                    ranks[to] = rank + 1
                    for x in range(2):
                        spot = rank * 2 + x
                        at = rows_at(spot // PER)
                        mine = kk[(u * 2 + x) * SHELL : (u * 2 + x + 1) * SHELL]
                        old = k_out[to, at, :]
                        k_out[to, at, :] = jnp.where(place == spot % PER, mine, old)
                    aim = blk_p // col_blocks
                    rank_c = ranks[n_row + aim]
                    ranks[n_row + aim] = rank_c + 1
                    way = lax.rem(aim - my_col + n_col, n_col)
                    at = rows_at(rank_c // PER)
                    mine = jj[u * SHELL : (u + 1) * SHELL]
                    for m in range(n_col):

                        @pl.when(way == m)
                        def _(m=m):
                            old = j_out[m][at, :]
                            j_out[m][at, :] = jnp.where(place == rank_c % PER, mine, old)

            return carry

        lax.fori_loop(0, steps, fold, 0)

    outs = call(
        body,
        in_specs=[vmem(), smem(), smem()] + [vmem()] * (1 + n_col),
        out_specs=[vmem()] * (1 + n_col),
        out_shape=[jax.ShapeDtypeStruct((n_row, rows_k, LANES), F32)]
        + [jax.ShapeDtypeStruct((rows_j, LANES), F32)] * n_col,
        scratch_shapes=[
            pltpu.VMEM((2, slots, SHELL, LANES), F32),
            pltpu.VMEM((slots, pair), F32),
            pltpu.VMEM((slots * 2 * SHELL, pair), F32),
            pltpu.VMEM((slots * SHELL, pair), F32),
            pltpu.VMEM((pair, pair), BF16),
            pltpu.SMEM((n_row + n_col,), I32),
        ],
        name="contract",
    )(integrals, tile_count, own, got_row, *got_col)
    return outs[0], outs[1:]


def stage(*arrays):
    size = len(arrays)

    def body(*refs):
        sems = refs[-1]
        moves = [pltpu.make_async_copy(refs[n], refs[size + n], sems.at[n]) for n in range(size)]
        for move in moves:
            move.start()
        for move in moves:
            move.wait()

    return call(
        body,
        in_specs=[pl.BlockSpec(memory_space=pltpu.HBM)] * size,
        out_specs=[vmem()] * size,
        out_shape=[jax.ShapeDtypeStruct(x.shape, x.dtype) for x in arrays],
        scratch_shapes=[pltpu.SemaphoreType.DMA((size,))],
        name="stage",
    )(*[pltpu.with_memory_space_constraint(x, pltpu.HBM) for x in arrays])


def plan(asked_row, asked_col, slots, row_blocks, col_blocks):
    n_row, n_col = asked_row.shape[0], len(asked_col)
    cap_row, cap_col = slots // n_row, slots // n_col
    total = n_row * cap_row + n_col * cap_col
    width = -(-(2 * total + 2) // LANES) * LANES

    def body(*refs):
        ask_row, ask_col, out = refs[0], refs[1 : 1 + n_col], refs[-1]
        my_row, my_col = lax.axis_index("row"), lax.axis_index("col")

        def note(spot, mine, row, col):
            spot = jnp.where(mine, spot, total)
            out[0, 2 * spot] = row
            out[0, 2 * spot + 1] = col
            return mine.astype(I32)

        def exchange(src, carry):
            rank = jnp.int32(0)
            for t in range(slots):
                blk_p = ask_row[src, t * 4] - my_row * row_blocks
                blk_r = ask_row[src, t * 4 + 2] - my_col * col_blocks
                mine = jnp.logical_and(blk_p >= 0, blk_p < row_blocks)
                rank = rank + note(src * cap_row + rank, mine, blk_p, blk_r)
            return carry

        lax.fori_loop(0, n_row, exchange, 0)
        for m in range(n_col):

            def coulomb(t, rank, m=m):
                blk_p = ask_col[m][0, t * 4] - my_col * col_blocks
                blk_q = ask_col[m][0, t * 4 + 1] - my_row * row_blocks
                mine = jnp.logical_and(blk_p >= 0, blk_p < col_blocks)
                return rank + note(n_row * cap_row + m * cap_col + rank, mine, blk_q, blk_p)

            lax.fori_loop(0, slots, coulomb, jnp.int32(0), unroll=8)

    return call(
        body,
        in_specs=[smem()] * (1 + n_col),
        out_specs=smem(),
        out_shape=jax.ShapeDtypeStruct((1, width), I32),
        name="plan",
    )(asked_row, *asked_col)


def assemble(k_got, j_got, where, slots, shape):
    n_row, n_col = k_got.shape[0], len(j_got)
    cap_row, cap_col = slots // n_row, slots // n_col

    def body(*refs):
        k_ref, where_ref = refs[:2]
        j_ref = refs[2 : 2 + n_col]
        out_a, out_b = refs[2 + n_col :]
        place = iota((SHELL, LANES), 1) // SHELL
        out_a[...] = jnp.zeros(shape, F32)
        out_b[...] = jnp.zeros(shape, F32)

        def spot_of(n):
            row, col = where_ref[0, 2 * n], where_ref[0, 2 * n + 1]
            return (rows_at(row), lanes_at(col)), col & (PER - 1)

        for m in range(n_col):
            for rank in range(cap_col):
                at, off = spot_of(n_row * cap_row + m * cap_col + rank)
                piece = turn(j_ref[m][rows_at(rank // PER), :], off, rank % PER)
                piece = jnp.where(place == off, piece, 0.0)
                out_a[at] = out_a[at] + piece
                out_b[at] = out_b[at] + piece
        for src in range(n_row):
            for rank in range(cap_row):
                at, off = spot_of(src * cap_row + rank)
                for x, out in ((0, out_a), (1, out_b)):
                    spot = rank * 2 + x
                    piece = turn(k_ref[src, rows_at(spot // PER), :], off, spot % PER)
                    out[at] = out[at] - jnp.where(place == off, piece, 0.0)

    return call(
        body,
        in_specs=[vmem(), smem()] + [vmem()] * n_col,
        out_specs=[vmem(), vmem()],
        out_shape=[jax.ShapeDtypeStruct(shape, F32)] * 2,
        name="assemble",
    )(k_got, where, *j_got)


def shift(x, step, size):
    return lax.ppermute(x, "col", [(n, (n + step) % size) for n in range(size)])


def swap(x):
    return lax.all_to_all(x, "row", split_axis=0, concat_axis=0, tiled=True)


def local(dens_alpha, dens_beta, integrals, tile_quartet, tile_count):
    slots = integrals.shape[0]
    n_row, n_col = lax.axis_size("row"), lax.axis_size("col")
    row_blocks, col_blocks = dens_alpha.shape[0] // SHELL, dens_alpha.shape[1] // SHELL
    live = jnp.arange(slots, dtype=I32)[:, None] < tile_count
    names_s = jnp.arange(4, dtype=I32)[None, :] == 3
    asks = jnp.where(jnp.logical_or(live, jnp.logical_not(names_s)), tile_quartet, -1)
    flat = asks.reshape(1, slots * 4)
    own = jnp.pad(flat, ((0, 0), (0, -(slots * 4) % LANES)))
    asked_col = [own] + [shift(own, m, n_col) for m in range(1, n_col)]
    asked_row = swap(jnp.broadcast_to(own, (n_row, own.shape[1])))
    alpha, beta, tiles = stage(dens_alpha, dens_beta, integrals)
    to_row, to_col = serve(alpha, beta, asked_row, asked_col, slots)
    got_col = [to_col[0]] + [shift(to_col[m], -m, n_col) for m in range(1, n_col)]
    got_row = swap(to_row)
    where = plan(asked_row, asked_col, slots, row_blocks, col_blocks)
    k_send, j_send = contract(tiles, tile_count, own, got_row, got_col, row_blocks, col_blocks)
    j_got = [j_send[0]] + [shift(j_send[m], m, n_col) for m in range(1, n_col)]
    k_got = swap(k_send)
    out_a, out_b = assemble(k_got, j_got, where, slots, dens_alpha.shape)
    return (out_a, out_b)


def solution(mesh):
    in_specs = (
        P("row", "col"),
        P("row", "col"),
        P(("row", "col"), None, None),
        P(("row", "col"), None),
        P(("row", "col")),
    )
    out_specs = (P("row", "col"), P("row", "col"))
    return jax.shard_map(local, mesh=mesh, in_specs=in_specs, out_specs=out_specs, check_vma=False)
```
